256 devices in a mesh: rows: 32 (over z, y), tab: 8 (over x, core).
Axes of the slice: x: 4, y: 4, z: 8, core: 2. Of those that a mesh axis runs over, the one named last changes fastest.
Arguments:
- vectors: bfloat16 [262144, 768], P(('rows', 'tab')), may hold values from -6 to 6
- list_owner: int32 [262144, 1], P(('rows', 'tab')), may hold values from 0 to 255; in each aligned block of 1024 rows (0 to 1023, 1024 to 2047, ...) at most 8 rows name the same one
- list_slot: int32 [262144], P(('rows', 'tab')), may hold values from 0 to 2047
- codes: int32 [262144, 96], P(('rows', 'tab')), may hold values from 0 to 255
- centroids: bfloat16 [524288, 768], P(('rows', 'tab')), may hold values from -6 to 6
- rotation: bfloat16 [768, 768], replicated, may hold values from -0.21875 to 0.21875
- old_codebooks: float32 [96, 8, 256], P('rows'), may hold values from -6 to 6
Outputs:
- codebooks: float32 [96, 8, 256], P('rows')
The draws below stay inside these ranges and needn't reach their ends.
Inputs may be any that keep to these rules, and one draw needn't show every extreme that they name: `list_owner`: among the rows of one device, at most 8 rows name the same value, and in every draw some device has exactly 8 rows naming one value.
All inputs are finite; a program needn't handle non-finite values.
Results may differ from the reference program's by a relative error of at most 0.0015.
Values may be sent and summed in bfloat16 or wider, within the bound.
A program may use at most 64 MiB of HBM per device.

```python
import math
import jax
import jax.numpy as jnp
import numpy as np
from jax import lax

D = 768
M = 96
K = 256
LIST_DEV = 2048
ROW_DEV = 1024
CAP = 8
ROWS = 262144
NLIST = 524288
DSUB = 8
N_ROWS = 32
N_TAB = 8
DEVICES = 256


def with_ends(drawn, key, low, high):
    extent = drawn.shape
    index_at = [jax.random.randint(jax.random.fold_in(key, axis), (), 0, extent[axis]) for axis in range(len(extent))]
    drawn = drawn.at[tuple(index_at)].set(low)
    longest = extent.index(max(extent))
    index_at[longest] = (index_at[longest] + 1) % extent[longest]
    return drawn.at[tuple(index_at)].set(high)


def level_of(stream_key, shape, cuts, low, top_value):
    level = 1.0
    for dim, blocks in cuts:
        draws = jax.random.uniform(jax.random.fold_in(jax.random.fold_in(stream_key, 6), dim), (blocks,), jnp.float32, low / len(cuts), top_value / len(cuts))
        level = level * jnp.repeat(jnp.exp(draws), shape[dim] // blocks).reshape((-1,) + (1,) * (len(shape) - 1 - dim))
    return level


def routed_block(own_key, own, number, rows, amount, top, most, skew):
    sequence = jax.random.permutation(own_key, amount)
    packed, usual = shares(amount, rows * top, most, skew, True), shares(amount, rows * top, most, skew, False)
    places = jnp.arange(amount)

    def named(sizes, turn):
        used = int((sizes > 0).sum())
        fixed = max(1, used // 4)
        moved = fixed + (places - fixed + turn * (used - fixed)) % max(1, amount - fixed)
        return jnp.zeros((amount,), jnp.int32).at[sequence[jnp.where(places < fixed, places, moved)]].set(jnp.asarray(sizes, jnp.int32))

    sizes = jnp.where(number % 4 == 0, named(packed, number // 4), named(usual, number - number // 4 - 1))
    mixed = jax.random.permutation(jax.random.fold_in(own, 3), amount)
    giver, receiver = mixed[0:amount // 2 * 2:2], mixed[1:amount // 2 * 2:2]
    room = jnp.minimum(sizes[giver] - 1, most - sizes[receiver]) // 2
    room = jnp.where((giver == sequence[0]) | (receiver == sequence[0]) | (sizes[receiver] == 0), 0, jnp.maximum(room, 0))
    moved = jax.random.randint(jax.random.fold_in(own, 4), (amount // 2,), 0, 1 << 20) % (room + 1)
    sizes = sizes.at[giver].add(-moved).at[receiver].add(moved)
    labels = jnp.searchsorted(jnp.cumsum(sizes), jnp.arange(rows * top), side="right").astype(jnp.int32)
    table = labels.reshape(top, rows).T
    table = table[jax.random.permutation(jax.random.fold_in(own, 1), rows)]
    turn = jax.random.randint(jax.random.fold_in(own, 2), (rows, 1), 0, top)
    return jnp.take_along_axis(table, (jnp.arange(top)[None, :] + turn) % top, axis=1)


def shares(count, total, limit, skew, full):
    weights = [(1 << 20) // math.isqrt(grade ** skew) + 1 for grade in range(1, count + 1)]
    largest = limit if full else min(limit, max(-(-total // count), total * weights[0] // sum(weights)))
    least = 1 if total - largest >= count - 1 else 0
    holding, rest = [largest] + [least] * (count - 1), total - largest - least * (count - 1)
    while rest > 0:
        movable = [i for i in range(1, count) if holding[i] < largest] or [i for i in range(1, count) if holding[i] < limit]
        whole, left = sum([weights[i] for i in movable]), rest
        for i in movable:
            addition = min(limit - holding[i], max(1, left * weights[i] // whole), rest)
            holding[i] = holding[i] + addition
            rest = rest - addition
    return np.array(holding)


def scatter_about(stream_key, shape, deviation, reach, pieces=(), held_as=jnp.bfloat16):
    drawn = jax.random.normal(stream_key, shape, jnp.float32) * deviation
    if len(pieces) > 0:
        drawn = level_of(stream_key, shape, pieces, -0.22, 0.18) * drawn
    return jnp.clip(drawn, min=-reach, max=reach).astype(held_as)


def setup_inputs(seed: int = 0) -> dict:
    arg_keys = jax.random.split(jax.random.key(seed), 8)
    vectors = scatter_about(arg_keys[0], (ROWS, D), 1.0, 6.0, ((0, 256),))
    list_owner_keys = jax.random.split(jax.random.fold_in(arg_keys[1], 1), ROWS // ROW_DEV)
    list_owner_turns = jax.random.permutation(jax.random.fold_in(arg_keys[1], 3), ROWS // ROW_DEV)
    list_owner = jax.vmap(lambda own, number: routed_block(jax.random.fold_in(arg_keys[1], 2), own, number, ROW_DEV, DEVICES, 1, CAP, 2))(list_owner_keys, list_owner_turns).reshape((ROWS, 1))
    list_slot = with_ends(jax.random.randint(arg_keys[2], (ROWS,), 0, LIST_DEV), jax.random.fold_in(arg_keys[2], 1), 0, LIST_DEV - 1).astype(jnp.int32)
    codes = with_ends(jax.random.randint(arg_keys[3], (ROWS, M), 0, K), jax.random.fold_in(arg_keys[3], 1), 0, K - 1).astype(jnp.int32)
    centroids = scatter_about(arg_keys[4], (NLIST, D), 1.0, 6.0, ((0, 256),))
    rotation = scatter_about(arg_keys[5], (D, D), D ** -0.5, 0.21875)
    old_codebooks = scatter_about(arg_keys[6], (M, DSUB, K), 1.0, 6.0, ((0, 32),), jnp.float32)
    return {"vectors": vectors, "list_owner": list_owner, "list_slot": list_slot, "codes": codes, "centroids": centroids, "rotation": rotation, "old_codebooks": old_codebooks}


def reference(vectors, list_owner, list_slot, codes, centroids, rotation, old_codebooks):
    blocks = N_ROWS * N_TAB
    sub_width = D // M
    owners_all = list_owner[:, 0]

    def accumulate(totals, index):
        word_sums, word_counts = totals
        offset = (index * ROW_DEV).astype(jnp.int32)
        row_block = lax.dynamic_slice_in_dim(vectors, offset, ROW_DEV, 0)
        owners = lax.dynamic_slice_in_dim(owners_all, offset, ROW_DEV, 0)
        slot_ids = lax.dynamic_slice_in_dim(list_slot, offset, ROW_DEV, 0)
        code_block = lax.dynamic_slice_in_dim(codes, offset, ROW_DEV, 0)
        picked = centroids[owners * LIST_DEV + slot_ids]
        centre_rot = jnp.dot(picked, rotation, preferred_element_type=jnp.float32).astype(jnp.bfloat16)
        data_rot = jnp.dot(row_block, rotation, preferred_element_type=jnp.float32).astype(jnp.bfloat16)
        segments = (code_block + jnp.arange(M, dtype=jnp.int32)[None, :] * K).reshape(-1)
        data_pieces = data_rot.astype(jnp.float32).reshape(ROW_DEV * M, sub_width)
        centre_pieces = centre_rot.astype(jnp.float32).reshape(ROW_DEV * M, sub_width)
        data_sums = jax.ops.segment_sum(data_pieces, segments, num_segments=M * K)
        centre_sums = jax.ops.segment_sum(centre_pieces, segments, num_segments=M * K)
        word_sums = word_sums + (data_sums - centre_sums)
        word_counts = word_counts + jax.ops.segment_sum(jnp.ones((ROW_DEV * M,), jnp.float32), segments, num_segments=M * K)
        return (word_sums, word_counts), None

    start_sums = jnp.zeros((M * K, sub_width), jnp.float32)
    start_counts = jnp.zeros((M * K,), jnp.float32)
    (word_sums, word_counts), _ = lax.scan(accumulate, (start_sums, start_counts), jnp.arange(blocks, dtype=jnp.int32))
    word_sums = word_sums.reshape(M, K, sub_width).transpose(0, 2, 1)
    word_counts = word_counts.reshape(M, K)[:, None, :]
    prior_weight = float(ROWS // K)
    return (word_sums + prior_weight * old_codebooks) / (word_counts + prior_weight)
```

```python
import functools

import jax
import jax.numpy as jnp
from jax import lax
from jax.experimental import pallas as pl
from jax.experimental.pallas import tpu as pltpu
from jax.sharding import PartitionSpec as P

FIELDS = 128
LOW = 32
BF16 = jnp.bfloat16
F32 = jnp.float32
I32 = jnp.int32
NT = (((1,), (1,)), ((), ()))


def iota(shape, axis):
    return lax.broadcasted_iota(I32, shape, axis)


def route_kernel(devices, owner_ref, slot_ref, codes_ref, message_ref):
    subspaces, rows = codes_ref.shape
    places = message_ref.shape[0]
    cap = places // devices
    owner = owner_ref[...]
    same = iota((devices, rows), 0) == owner
    before = (iota((rows, rows), 0) < iota((rows, rows), 1)).astype(F32).astype(BF16)
    rank = jnp.dot(same.astype(F32).astype(BF16), before, preferred_element_type=F32)
    rank = jnp.sum(jnp.where(same, rank, 0.0), axis=0, keepdims=True)
    place = owner * cap + rank.astype(I32)
    slot = slot_ref[...]
    line = iota((FIELDS - subspaces, rows), 0)
    extra = jnp.where(line == 0, slot >> 4, jnp.where(line == 1, slot & 15, (line == 2).astype(I32)))
    info = jnp.concatenate([codes_ref[...], extra], axis=0).astype(F32).astype(BF16)
    step = 256
    for start in range(0, places, step):
        hit = ((iota((step, rows), 0) + start) == place).astype(F32).astype(BF16)
        message_ref[start : start + step, :] = lax.dot_general(
            hit, info, NT, preferred_element_type=F32
        ).astype(BF16)


def sums_kernel(
    vectors_ref, codes_ref, requests_ref, centroids_ref, rotation_ref,
    sums_ref, counts_ref,
    parts, high, low, left, right, turned, flipped,
):
    subspaces, rows = codes_ref.shape
    lists, width = centroids_ref.shape
    asked = requests_ref.shape[0]
    total = rows + asked
    sub_width = width // subspaces
    codewords = sums_ref.shape[1]
    top = codewords // LOW

    unit = (iota((256, width), 0) == iota((256, width), 1)).astype(F32).astype(BF16)
    for start in range(0, width, 256):
        picker = ((iota((256, width), 0) + start) == iota((256, width), 1)).astype(F32).astype(BF16)
        flipped[start : start + 256, :] = lax.dot_general(
            picker, rotation_ref[...], NT, preferred_element_type=F32
        ).astype(BF16)
    for start in range(0, rows, 256):
        parts[:, start : start + 256] = lax.dot_general(
            flipped[...], vectors_ref[start : start + 256, :], NT, preferred_element_type=F32
        ).astype(BF16)
    for start in range(0, lists, 256):
        turned[:, start : start + 256] = lax.dot_general(
            flipped[...], centroids_ref[start : start + 256, :], NT, preferred_element_type=F32
        ).astype(BF16)

    codes = codes_ref[...]
    high[:, :rows] = (codes >> 5).astype(F32)
    low[:, :rows] = (codes & (LOW - 1)).astype(F32)
    step = 256
    small = unit[:FIELDS, :FIELDS]
    for start in range(0, asked, step):
        fields = lax.dot_general(
            small, requests_ref[start : start + step, :], NT, preferred_element_type=F32
        ).astype(I32)
        valid = fields[subspaces + 2 : subspaces + 3, :] > 0
        slot = fields[subspaces : subspaces + 1, :] * 16 + fields[subspaces + 1 : subspaces + 2, :]
        asked_codes = fields[:subspaces, :]
        here = slice(rows + start, rows + start + step)
        high[:, here] = jnp.where(valid, asked_codes >> 5, top + 1).astype(F32)
        low[:, here] = (asked_codes & (LOW - 1)).astype(F32)
        pick = (iota((lists, step), 0) == slot).astype(F32).astype(BF16)
        parts[:, here] = (-jnp.dot(turned[...], pick, preferred_element_type=F32)).astype(BF16)

    group = codewords // LOW
    lines = group * sub_width
    chunk = 512

    def one_group(index, carry):
        line = pl.multiple_of(index * group, group)
        wide = pl.multiple_of(index * lines, lines)
        for start in range(0, total, chunk):
            here = slice(start, start + chunk)
            high8 = high[pl.ds(line, group), here]
            low8 = low[pl.ds(line, group), here]
            piece = parts[pl.ds(wide, lines), here]
            spread = jnp.concatenate(
                [jnp.broadcast_to(high8[m : m + 1], (sub_width, chunk)) for m in range(group)], axis=0
            ).astype(BF16)
            for value in range(top):
                left[value * lines : (value + 1) * lines, here] = jnp.where(
                    spread == jnp.array(value, BF16), piece, jnp.zeros_like(piece)
                )
            row_id = iota((LOW, chunk), 0).astype(F32).astype(BF16)
            for m in range(group):
                row = jnp.broadcast_to(low8[m : m + 1], (LOW, chunk)).astype(BF16)
                right[m * LOW : (m + 1) * LOW, here] = jnp.where(
                    row == row_id, jnp.array(1, BF16), jnp.array(0, BF16)
                )
        crossed = lax.dot_general(left[...], right[...], NT, preferred_element_type=F32)
        high8 = high[pl.ds(line, group), :rows]
        marks = jnp.concatenate(
            [jnp.where(high8 == float(value), 1.0, 0.0) for value in range(top)], axis=0
        ).astype(BF16)
        tally = lax.dot_general(marks, right[:, :rows], NT, preferred_element_type=F32)

        def fold(crossing, count, per):
            owner = iota((count, codewords), 0) // per
            keep = owner == iota((count, codewords), 1) // LOW
            halves = [jnp.zeros((count, 128), F32) for _ in range(codewords // 128)]
            lane = iota((count, 128), 1) // LOW
            for value in range(top):
                block = jnp.where(keep, crossing[value * count : (value + 1) * count, :], 0.0)
                line_sum = block[:, :128] + block[:, 128:]
                line_sum = line_sum + pltpu.roll(line_sum, 64, 1)
                line_sum = line_sum + pltpu.roll(line_sum, 32, 1)
                at = value // 4
                halves[at] = halves[at] + jnp.where(lane == value % 4, line_sum, 0.0)
            return jnp.concatenate(halves, axis=1)

        sums_ref[pl.ds(wide, lines), :] = fold(crossed, lines, sub_width)
        counts_ref[pl.ds(line, group), :] = fold(tally, group, 1)
        return carry

    lax.fori_loop(0, subspaces // group, one_group, 0)


def in_vmem(count):
    return [pl.BlockSpec(memory_space=pltpu.VMEM)] * count


def route(owner, slot, codes_t, devices):
    rows = owner.shape[1]
    places = 2 * rows
    return pl.pallas_call(
        functools.partial(route_kernel, devices),
        out_shape=jax.ShapeDtypeStruct((places, FIELDS), BF16),
        in_specs=in_vmem(3),
        out_specs=pl.BlockSpec(memory_space=pltpu.VMEM),
    )(owner, slot, codes_t)


def local_sums(vectors, codes_t, requests, centroids, rotation, codewords):
    subspaces, rows = codes_t.shape
    lists, width = centroids.shape
    asked = requests.shape[0]
    total = rows + asked
    top = codewords // LOW
    return pl.pallas_call(
        sums_kernel,
        out_shape=[
            jax.ShapeDtypeStruct((width, codewords), F32),
            jax.ShapeDtypeStruct((subspaces, codewords), F32),
        ],
        in_specs=in_vmem(5),
        out_specs=in_vmem(2),
        scratch_shapes=[
            pltpu.VMEM((width, total), BF16),
            pltpu.VMEM((subspaces, total), F32),
            pltpu.VMEM((subspaces, total), F32),
            pltpu.VMEM((top * 64, total), BF16),
            pltpu.VMEM((codewords, total), BF16),
            pltpu.VMEM((width, lists), BF16),
            pltpu.VMEM((width, width), BF16),
        ],
    )(vectors, codes_t, requests, centroids, rotation)


def body(vectors, list_owner, list_slot, codes, centroids, rotation, old_codebooks):
    n_rows = lax.axis_size("rows")
    n_tab = lax.axis_size("tab")
    devices = n_rows * n_tab
    row_dev, width = vectors.shape
    own, sub_width, codewords = old_codebooks.shape
    cap = 2 * row_dev // devices
    codes_t = codes.T
    message = route(list_owner.reshape(1, row_dev), list_slot.reshape(1, row_dev), codes_t, devices)
    message = message.reshape(n_rows, n_tab, cap, FIELDS)
    message = lax.all_to_all(message, "rows", split_axis=0, concat_axis=0, tiled=True)
    message = lax.all_to_all(message, "tab", split_axis=1, concat_axis=1, tiled=True)
    requests = message.reshape(devices * cap, FIELDS)
    sums, counts = local_sums(vectors, codes_t, requests, centroids, rotation, codewords)
    coarse = jnp.floor(counts * (1 / 256)) * 256
    tallies = jnp.stack([coarse, counts - coarse], axis=1)
    share = jnp.concatenate(
        [sums.reshape(n_rows * own, sub_width, codewords), tallies], axis=1
    ).astype(BF16)
    share = share.reshape(n_rows, own * (sub_width + 2), codewords)
    share = lax.all_to_all(share, "rows", split_axis=0, concat_axis=0, tiled=True)
    share = jnp.sum(share.astype(F32), axis=0)
    share = lax.psum(share, "tab").reshape(own, sub_width + 2, codewords)
    word_sums = share[:, :sub_width]
    word_counts = share[:, sub_width] + share[:, sub_width + 1]
    prior = float(row_dev * devices // codewords)
    return (word_sums + prior * old_codebooks) / (word_counts[:, None, :] + prior)


def solution(mesh):
    return jax.shard_map(
        body,
        mesh=mesh,
        in_specs=(
            P(("rows", "tab"), None),
            P(("rows", "tab"), None),
            P(("rows", "tab")),
            P(("rows", "tab"), None),
            P(("rows", "tab"), None),
            P(),
            P("rows", None, None),
        ),
        out_specs=P("rows", None, None),
        check_vma=False,
    )
```

```python
import functools

import jax
import jax.numpy as jnp
from jax import lax
from jax.experimental import pallas as pl
from jax.experimental.pallas import tpu as pltpu
from jax.sharding import PartitionSpec as P

FIELDS = 128
LOW = 32
BF16 = jnp.bfloat16
F32 = jnp.float32
I32 = jnp.int32
NT = (((1,), (1,)), ((), ()))
MESH = pl.DeviceIdType.MESH


def iota(shape, axis):
    return lax.broadcasted_iota(I32, shape, axis)


def route_kernel(n_rows, n_tab, owner_ref, slot_ref, codes_ref, arrived_ref, message, arrived, sent_sem, got_sem):
    devices = n_rows * n_tab
    my_row, my_tab = lax.axis_index("rows"), lax.axis_index("tab")
    me = my_row * n_tab + my_tab
    barrier = pltpu.get_barrier_semaphore()

    def greet(offset, carry):
        peer = lax.rem(me + offset, devices)
        pl.semaphore_signal(
            barrier, inc=1, device_id=(peer // n_tab, lax.rem(peer, n_tab)), device_id_type=MESH
        )
        return carry

    lax.fori_loop(1, devices, greet, 0)
    subspaces, rows = codes_ref.shape
    cap = message.shape[1]
    owner = owner_ref[...]
    same = iota((devices, rows), 0) == owner
    before = (iota((rows, rows), 0) < iota((rows, rows), 1)).astype(F32).astype(BF16)
    rank = jnp.dot(same.astype(F32).astype(BF16), before, preferred_element_type=F32)
    rank = jnp.sum(jnp.where(same, rank, 0.0), axis=0, keepdims=True)
    place = owner * cap + rank.astype(I32)
    slot = slot_ref[...]
    line = iota((FIELDS - subspaces, rows), 0)
    extra = jnp.where(line == 0, slot >> 4, jnp.where(line == 1, slot & 15, (line == 2).astype(I32)))
    info = jnp.concatenate([codes_ref[...], extra], axis=0).astype(F32).astype(BF16)
    step = min(256, devices * cap)
    for start in range(0, devices * cap, step):
        hit = ((iota((step, rows), 0) + start) == place).astype(F32).astype(BF16)
        piece = lax.dot_general(hit, info, NT, preferred_element_type=F32).astype(BF16)
        message[start // cap : (start + step) // cap] = piece.reshape(step // cap, cap, FIELDS)
    arrived[me] = message[me]
    pl.semaphore_wait(barrier, devices - 1)

    def send(offset, carry):
        peer = lax.rem(me + offset, devices)
        pltpu.make_async_remote_copy(
            src_ref=message.at[peer],
            dst_ref=arrived.at[me],
            send_sem=sent_sem,
            recv_sem=got_sem,
            device_id=(peer // n_tab, lax.rem(peer, n_tab)),
            device_id_type=MESH,
        ).start()
        return carry

    lax.fori_loop(1, devices, send, 0)
    everything = pltpu.make_async_remote_copy(
        src_ref=message.at[pl.ds(0, devices - 1)],
        dst_ref=arrived.at[pl.ds(0, devices - 1)],
        send_sem=sent_sem,
        recv_sem=got_sem,
        device_id=(my_row, lax.rem(my_tab + 1, n_tab)),
        device_id_type=MESH,
    )
    everything.wait_recv()
    arrived_ref[...] = arrived[...].reshape(devices * cap, FIELDS)
    everything.wait_send()


def sums_kernel(
    vectors_ref, codes_ref, requests_ref, centroids_ref, rotation_ref,
    pieces_ref,
    sums_ref, counts_ref, parts, high, low, left, right, turned, flipped,
):
    subspaces, rows = codes_ref.shape
    lists, width = centroids_ref.shape
    asked = requests_ref.shape[0]
    total = rows + asked
    sub_width = width // subspaces
    codewords = sums_ref.shape[1]
    top = codewords // LOW

    unit = (iota((256, width), 0) == iota((256, width), 1)).astype(F32).astype(BF16)
    for start in range(0, width, 256):
        picker = ((iota((256, width), 0) + start) == iota((256, width), 1)).astype(F32).astype(BF16)
        flipped[start : start + 256, :] = lax.dot_general(
            picker, rotation_ref[...], NT, preferred_element_type=F32
        ).astype(BF16)
    for start in range(0, rows, 256):
        parts[:, start : start + 256] = lax.dot_general(
            flipped[...], vectors_ref[start : start + 256, :], NT, preferred_element_type=F32
        ).astype(BF16)
    for start in range(0, lists, 256):
        turned[:, start : start + 256] = lax.dot_general(
            flipped[...], centroids_ref[start : start + 256, :], NT, preferred_element_type=F32
        ).astype(BF16)

    codes = codes_ref[...]
    high[:, :rows] = (codes >> 5).astype(F32)
    low[:, :rows] = (codes & (LOW - 1)).astype(F32)
    step = 256
    small = unit[:FIELDS, :FIELDS]
    for start in range(0, asked, step):
        fields = lax.dot_general(
            small, requests_ref[start : start + step, :], NT, preferred_element_type=F32
        ).astype(I32)
        valid = fields[subspaces + 2 : subspaces + 3, :] > 0
        slot = fields[subspaces : subspaces + 1, :] * 16 + fields[subspaces + 1 : subspaces + 2, :]
        asked_codes = fields[:subspaces, :]
        here = slice(rows + start, rows + start + step)
        high[:, here] = jnp.where(valid, asked_codes >> 5, top + 1).astype(F32)
        low[:, here] = (asked_codes & (LOW - 1)).astype(F32)
        pick = (iota((lists, step), 0) == slot).astype(F32).astype(BF16)
        parts[:, here] = (-jnp.dot(turned[...], pick, preferred_element_type=F32)).astype(BF16)

    group = codewords // LOW
    lines = group * sub_width
    chunk = 512

    def one_group(index, carry):
        line = pl.multiple_of(index * group, group)
        wide = pl.multiple_of(index * lines, lines)
        for start in range(0, total, chunk):
            here = slice(start, start + chunk)
            high8 = high[pl.ds(line, group), here]
            low8 = low[pl.ds(line, group), here]
            piece = parts[pl.ds(wide, lines), here]
            spread = jnp.concatenate(
                [jnp.broadcast_to(high8[m : m + 1], (sub_width, chunk)) for m in range(group)], axis=0
            ).astype(BF16)
            for value in range(top):
                left[value * lines : (value + 1) * lines, here] = jnp.where(
                    spread == jnp.array(value, BF16), piece, jnp.zeros_like(piece)
                )
            row_id = iota((LOW, chunk), 0).astype(F32).astype(BF16)
            for m in range(group):
                row = jnp.broadcast_to(low8[m : m + 1], (LOW, chunk)).astype(BF16)
                right[m * LOW : (m + 1) * LOW, here] = jnp.where(
                    row == row_id, jnp.array(1, BF16), jnp.array(0, BF16)
                )
        crossed = lax.dot_general(left[...], right[...], NT, preferred_element_type=F32)
        high8 = high[pl.ds(line, group), :rows]
        marks = jnp.concatenate(
            [jnp.where(high8 == float(value), 1.0, 0.0) for value in range(top)], axis=0
        ).astype(BF16)
        tally = lax.dot_general(marks, right[:, :rows], NT, preferred_element_type=F32)

        def fold(crossing, count, per):
            owner = iota((count, codewords), 0) // per
            keep = owner == iota((count, codewords), 1) // LOW
            halves = [jnp.zeros((count, 128), F32) for _ in range(codewords // 128)]
            lane = iota((count, 128), 1) // LOW
            for value in range(top):
                block = jnp.where(keep, crossing[value * count : (value + 1) * count, :], 0.0)
                line_sum = block[:, :128] + block[:, 128:]
                line_sum = line_sum + pltpu.roll(line_sum, 64, 1)
                line_sum = line_sum + pltpu.roll(line_sum, 32, 1)
                at = value // 4
                halves[at] = halves[at] + jnp.where(lane == value % 4, line_sum, 0.0)
            return jnp.concatenate(halves, axis=1)

        sums_ref[pl.ds(wide, lines), :] = fold(crossed, lines, sub_width)
        counts_ref[pl.ds(line, group), :] = fold(tally, group, 1)
        return carry

    lax.fori_loop(0, subspaces // group, one_group, 0)

    n_rows = pieces_ref.shape[1]
    own = subspaces // n_rows
    counts = counts_ref[...]
    coarse = jnp.floor(counts * (1 / 256)) * 256
    fine = counts - coarse
    gap = jnp.zeros((8 - 2 * own, 128), F32)
    for r in range(n_rows):
        mine = slice(r * own, (r + 1) * own)
        for half in range(codewords // 128):
            lanes = slice(half * 128, (half + 1) * 128)
            for q in range(own):
                at = (r * own + q) * sub_width
                pieces_ref[2 * q + half, r] = sums_ref[at : at + sub_width, lanes].astype(BF16)
            pieces_ref[2 * own + half, r] = jnp.concatenate(
                [coarse[mine, lanes], fine[mine, lanes], gap], axis=0
            ).astype(BF16)


def collect_kernel(
    n_rows, n_tab, prior, pieces_ref, old_ref, out_ref,
    first, total, middle, second, mine, third,
    sent1, got1, sent2, got2, sent3, got3,
):
    my_row, my_tab = lax.axis_index("rows"), lax.axis_index("tab")
    barrier = pltpu.get_barrier_semaphore()

    def row_peer(offset):
        return lax.rem(my_row + offset, n_rows)

    def tab_peer(offset):
        return lax.rem(my_tab + offset, n_tab)

    def greet_row(offset, carry):
        pl.semaphore_signal(barrier, inc=1, device_id=(row_peer(offset), my_tab), device_id_type=MESH)
        return carry

    def greet_tab(offset, carry):
        pl.semaphore_signal(barrier, inc=1, device_id=(my_row, tab_peer(offset)), device_id_type=MESH)
        return carry

    lax.fori_loop(1, n_tab, greet_tab, 0)
    lax.fori_loop(1, n_rows, greet_row, 0)
    pl.semaphore_wait(barrier, n_rows + n_tab - 2)

    def copy1(source, slot, peer):
        return pltpu.make_async_remote_copy(
            src_ref=pieces_ref.at[source], dst_ref=first.at[slot],
            send_sem=sent1.at[source], recv_sem=got1.at[slot],
            device_id=(my_row, peer), device_id_type=MESH,
        )

    def start1(offset, carry):
        copy1(tab_peer(offset), my_tab, tab_peer(offset)).start()
        return carry

    lax.fori_loop(1, n_tab, start1, 0)
    total[...] = pieces_ref[my_tab].astype(F32)

    def add1(offset, carry):
        source = tab_peer(n_tab - offset)
        copy1(tab_peer(offset), source, tab_peer(offset)).wait_recv()
        total[...] += first[source].astype(F32)
        return carry

    lax.fori_loop(1, n_tab, add1, 0)
    middle[...] = total[...].astype(BF16)

    def copy2(source, slot, peer):
        return pltpu.make_async_remote_copy(
            src_ref=middle.at[source], dst_ref=second.at[slot],
            send_sem=sent2.at[source], recv_sem=got2.at[slot],
            device_id=(peer, my_tab), device_id_type=MESH,
        )

    def start2(offset, carry):
        copy2(row_peer(offset), my_row, row_peer(offset)).start()
        return carry

    lax.fori_loop(1, n_rows, start2, 0)

    def add2(offset, held):
        source = row_peer(n_rows - offset)
        copy2(row_peer(offset), source, row_peer(offset)).wait_recv()
        return held + second[source].astype(F32)

    mine[...] = lax.fori_loop(1, n_rows, add2, total[my_row])
    third[my_tab] = mine[...]

    def copy3(slot, peer):
        return pltpu.make_async_remote_copy(
            src_ref=mine, dst_ref=third.at[slot],
            send_sem=sent3.at[peer], recv_sem=got3.at[slot],
            device_id=(my_row, peer), device_id_type=MESH,
        )

    def start3(offset, carry):
        copy3(my_tab, tab_peer(offset)).start()
        return carry

    lax.fori_loop(1, n_tab, start3, 0)

    def wait3(offset, carry):
        copy3(tab_peer(n_tab - offset), tab_peer(offset)).wait_recv()
        return carry

    lax.fori_loop(1, n_tab, wait3, 0)
    own = out_ref.shape[0]
    for half in range(out_ref.shape[2] // 128):
        lanes = slice(half * 128, (half + 1) * 128)
        counts = third[2 * own + half]
        for q in range(own):
            weight = counts[q : q + 1] + counts[own + q : own + q + 1] + prior
            out_ref[q, :, lanes] = (third[2 * q + half] + prior * old_ref[q, :, lanes]) / weight

    def drain_tab(offset, carry):
        copy1(tab_peer(offset), my_tab, tab_peer(offset)).wait_send()
        copy3(my_tab, tab_peer(offset)).wait_send()
        return carry

    def drain_row(offset, carry):
        copy2(row_peer(offset), my_row, row_peer(offset)).wait_send()
        return carry

    lax.fori_loop(1, n_tab, drain_tab, 0)
    lax.fori_loop(1, n_rows, drain_row, 0)


def in_vmem(count):
    return [pl.BlockSpec(memory_space=pltpu.VMEM)] * count


def route(owner, slot, codes_t, n_rows, n_tab):
    rows = owner.shape[1]
    devices = n_rows * n_tab
    places = 2 * rows
    cap = places // devices
    return pl.pallas_call(
        functools.partial(route_kernel, n_rows, n_tab),
        out_shape=jax.ShapeDtypeStruct((places, FIELDS), BF16),
        in_specs=in_vmem(3),
        out_specs=pl.BlockSpec(memory_space=pltpu.VMEM),
        scratch_shapes=[
            pltpu.VMEM((devices, cap, FIELDS), BF16),
            pltpu.VMEM((devices, cap, FIELDS), BF16),
            pltpu.SemaphoreType.DMA,
            pltpu.SemaphoreType.DMA,
        ],
        compiler_params=pltpu.CompilerParams(collective_id=0, has_side_effects=True),
    )(owner, slot, codes_t)


def local_sums(vectors, codes_t, requests, centroids, rotation, codewords, n_rows):
    subspaces, rows = codes_t.shape
    lists, width = centroids.shape
    asked = requests.shape[0]
    total = rows + asked
    top = codewords // LOW
    return pl.pallas_call(
        sums_kernel,
        out_shape=jax.ShapeDtypeStruct(
            ((subspaces // n_rows + 1) * (codewords // 128), n_rows, 8, 128), BF16
        ),
        in_specs=in_vmem(5),
        out_specs=pl.BlockSpec(memory_space=pltpu.VMEM),
        scratch_shapes=[
            pltpu.VMEM((width, codewords), F32),
            pltpu.VMEM((subspaces, codewords), F32),
            pltpu.VMEM((width, total), BF16),
            pltpu.VMEM((subspaces, total), F32),
            pltpu.VMEM((subspaces, total), F32),
            pltpu.VMEM((top * 64, total), BF16),
            pltpu.VMEM((codewords, total), BF16),
            pltpu.VMEM((width, lists), BF16),
            pltpu.VMEM((width, width), BF16),
        ],
    )(vectors, codes_t, requests, centroids, rotation)


def collect(pieces, old_codebooks, prior, n_rows, n_tab):
    piece = pieces.shape[2:]
    return pl.pallas_call(
        functools.partial(collect_kernel, n_rows, n_tab, prior),
        out_shape=jax.ShapeDtypeStruct(old_codebooks.shape, F32),
        in_specs=in_vmem(2),
        out_specs=pl.BlockSpec(memory_space=pltpu.VMEM),
        scratch_shapes=[
            pltpu.VMEM((n_tab, n_rows, *piece), BF16),
            pltpu.VMEM((n_rows, *piece), F32),
            pltpu.VMEM((n_rows, *piece), BF16),
            pltpu.VMEM((n_rows, *piece), BF16),
            pltpu.VMEM(piece, F32),
            pltpu.VMEM((n_tab, *piece), F32),
            pltpu.SemaphoreType.DMA((n_tab,)),
            pltpu.SemaphoreType.DMA((n_tab,)),
            pltpu.SemaphoreType.DMA((n_rows,)),
            pltpu.SemaphoreType.DMA((n_rows,)),
            pltpu.SemaphoreType.DMA((n_tab,)),
            pltpu.SemaphoreType.DMA((n_tab,)),
        ],
        compiler_params=pltpu.CompilerParams(collective_id=1, has_side_effects=True),
    )(pieces, old_codebooks)


def body(vectors, list_owner, list_slot, codes, centroids, rotation, old_codebooks):
    n_rows = lax.axis_size("rows")
    n_tab = lax.axis_size("tab")
    devices = n_rows * n_tab
    row_dev, width = vectors.shape
    codewords = old_codebooks.shape[2]
    codes_t = codes.T
    requests = route(
        list_owner.reshape(1, row_dev), list_slot.reshape(1, row_dev), codes_t, n_rows, n_tab
    )
    pieces = local_sums(vectors, codes_t, requests, centroids, rotation, codewords, n_rows)
    prior = float(row_dev * devices // codewords)
    return collect(pieces, old_codebooks, prior, n_rows, n_tab)


def solution(mesh):
    return jax.shard_map(
        body,
        mesh=mesh,
        in_specs=(
            P(("rows", "tab"), None),
            P(("rows", "tab"), None),
            P(("rows", "tab")),
            P(("rows", "tab"), None),
            P(("rows", "tab"), None),
            P(),
            P("rows", None, None),
        ),
        out_specs=P("rows", None, None),
        check_vma=False,
    )
```

```python
import functools

import jax
import jax.numpy as jnp
from jax import lax
from jax.experimental import pallas as pl
from jax.experimental.pallas import tpu as pltpu
from jax.sharding import PartitionSpec as P

FIELDS = 128
LOW = 32
BF16 = jnp.bfloat16
F32 = jnp.float32
I32 = jnp.int32
NT = (((1,), (1,)), ((), ()))
MESH = pl.DeviceIdType.MESH


def iota(shape, axis):
    return lax.broadcasted_iota(I32, shape, axis)


def fused_kernel(
    n_rows, n_tab,
    owner_ref, slot_ref, codes_ref, vectors_hbm, centroids_hbm, rotation_hbm,
    out_ref,
    vectors_ref, centroids_ref, rotation_ref, load_sem,
    message, arrived, sent_sem, got_sem,
    sums, tallies, parts, high, low, left, right, turned, flipped,
    pieces, first, total, middle, second, mine, third,
    sent1, got1, sent2, got2, sent3, got3,
):
    devices = n_rows * n_tab
    my_row, my_tab = lax.axis_index("rows"), lax.axis_index("tab")
    me = my_row * n_tab + my_tab
    barrier = pltpu.get_barrier_semaphore()

    loads = [
        pltpu.make_async_copy(source, target, load_sem.at[number])
        for number, (source, target) in enumerate(
            [(rotation_hbm, rotation_ref), (vectors_hbm, vectors_ref), (centroids_hbm, centroids_ref)]
        )
    ]
    for load in loads:
        load.start()

    def greet(offset, carry):
        peer = lax.rem(me + offset, devices)
        pl.semaphore_signal(
            barrier, inc=1, device_id=(peer // n_tab, lax.rem(peer, n_tab)), device_id_type=MESH
        )
        return carry

    lax.fori_loop(1, devices, greet, 0)

    subspaces, rows = codes_ref.shape
    cap = message.shape[1]
    owner = owner_ref[...]
    same = iota((devices, rows), 0) == owner
    before = (iota((rows, rows), 0) < iota((rows, rows), 1)).astype(F32).astype(BF16)
    rank = jnp.dot(same.astype(F32).astype(BF16), before, preferred_element_type=F32)
    rank = jnp.sum(jnp.where(same, rank, 0.0), axis=0, keepdims=True)
    place = owner * cap + rank.astype(I32)
    slot = slot_ref[...]
    line = iota((FIELDS - subspaces, rows), 0)
    extra = jnp.where(line == 0, slot >> 4, jnp.where(line == 1, slot & 15, (line == 2).astype(I32)))
    info = jnp.concatenate([codes_ref[...], extra], axis=0).astype(F32).astype(BF16)
    step = min(256, devices * cap)
    for start in range(0, devices * cap, step):
        hit = ((iota((step, rows), 0) + start) == place).astype(F32).astype(BF16)
        piece = lax.dot_general(hit, info, NT, preferred_element_type=F32).astype(BF16)
        message[start // cap : (start + step) // cap] = piece.reshape(step // cap, cap, FIELDS)
    arrived[me] = message[me]
    pl.semaphore_wait(barrier, devices - 1)

    def send(offset, carry):
        peer = lax.rem(me + offset, devices)
        pltpu.make_async_remote_copy(
            src_ref=message.at[peer],
            dst_ref=arrived.at[me],
            send_sem=sent_sem,
            recv_sem=got_sem,
            device_id=(peer // n_tab, lax.rem(peer, n_tab)),
            device_id_type=MESH,
        ).start()
        return carry

    lax.fori_loop(1, devices, send, 0)

    lists, width = centroids_ref.shape
    asked = devices * cap
    sub_width = width // subspaces
    codewords = sums.shape[1]
    top = codewords // LOW
    group = codewords // LOW
    lines = group * sub_width

    codes = codes_ref[...]
    high[:, :rows] = (codes >> 5).astype(F32)
    low[:, :rows] = (codes & (LOW - 1)).astype(F32)
    loads[0].wait()
    for start in range(0, width, 256):
        picker = ((iota((256, width), 0) + start) == iota((256, width), 1)).astype(F32).astype(BF16)
        flipped[start : start + 256, :] = lax.dot_general(
            picker, rotation_ref[...], NT, preferred_element_type=F32
        ).astype(BF16)
    loads[1].wait()
    for start in range(0, rows, 256):
        parts[:, start : start + 256] = lax.dot_general(
            flipped[...], vectors_ref[start : start + 256, :], NT, preferred_element_type=F32
        ).astype(BF16)

    def fill(index, begin, end):
        line = pl.multiple_of(index * group, group)
        wide = pl.multiple_of(index * lines, lines)
        chunk = 512
        for start in range(begin, end, chunk):
            here = slice(start, start + chunk)
            high8 = high[pl.ds(line, group), here]
            low8 = low[pl.ds(line, group), here]
            piece = parts[pl.ds(wide, lines), here]
            spread = jnp.concatenate(
                [jnp.broadcast_to(high8[m : m + 1], (sub_width, chunk)) for m in range(group)], axis=0
            ).astype(BF16)
            for value in range(top):
                left[value * lines : (value + 1) * lines, here] = jnp.where(
                    spread == jnp.array(value, BF16), piece, jnp.zeros_like(piece)
                )
            row_id = iota((LOW, chunk), 0).astype(F32).astype(BF16)
            for m in range(group):
                row = jnp.broadcast_to(low8[m : m + 1], (LOW, chunk)).astype(BF16)
                right[m * LOW : (m + 1) * LOW, here] = jnp.where(
                    row == row_id, jnp.array(1, BF16), jnp.array(0, BF16)
                )
        return lax.dot_general(
            left[:, begin:end], right[:, begin:end], NT, preferred_element_type=F32
        )

    def fold(crossing, count, per):
        keep = iota((count, codewords), 0) // per == iota((count, codewords), 1) // LOW
        halves = [jnp.zeros((count, 128), F32) for _ in range(codewords // 128)]
        lane = iota((count, 128), 1) // LOW
        for value in range(top):
            block = jnp.where(keep, crossing[value * count : (value + 1) * count, :], 0.0)
            line_sum = block[:, :128] + block[:, 128:]
            line_sum = line_sum + pltpu.roll(line_sum, 64, 1)
            line_sum = line_sum + pltpu.roll(line_sum, 32, 1)
            at = value // 4
            halves[at] = halves[at] + jnp.where(lane == value % 4, line_sum, 0.0)
        return jnp.concatenate(halves, axis=1)

    def own_group(index, carry):
        line = pl.multiple_of(index * group, group)
        wide = pl.multiple_of(index * lines, lines)
        crossed = fill(index, 0, rows)
        high8 = high[pl.ds(line, group), :rows]
        marks = jnp.concatenate(
            [jnp.where(high8 == float(value), 1.0, 0.0) for value in range(top)], axis=0
        ).astype(BF16)
        tally = lax.dot_general(marks, right[:, :rows], NT, preferred_element_type=F32)
        sums[pl.ds(wide, lines), :] = fold(crossed, lines, sub_width)
        tallies[pl.ds(line, group), :] = fold(tally, group, 1)
        return carry

    lax.fori_loop(0, subspaces // group, own_group, 0)
    loads[2].wait()
    for start in range(0, lists, 256):
        turned[:, start : start + 256] = lax.dot_general(
            flipped[...], centroids_ref[start : start + 256, :], NT, preferred_element_type=F32
        ).astype(BF16)
    own = subspaces // n_rows
    counts = tallies[...]
    coarse = jnp.floor(counts * (1 / 256)) * 256
    fine = counts - coarse
    gap = jnp.zeros((8 - 2 * own, 128), F32)
    for r in range(n_rows):
        these = slice(r * own, (r + 1) * own)
        for half in range(codewords // 128):
            lanes = slice(half * 128, (half + 1) * 128)
            pieces[2 * own + half, r] = jnp.concatenate(
                [coarse[these, lanes], fine[these, lanes], gap], axis=0
            ).astype(BF16)

    everything = pltpu.make_async_remote_copy(
        src_ref=message.at[pl.ds(0, devices - 1)],
        dst_ref=arrived.at[pl.ds(0, devices - 1)],
        send_sem=sent_sem,
        recv_sem=got_sem,
        device_id=(my_row, lax.rem(my_tab + 1, n_tab)),
        device_id_type=MESH,
    )
    everything.wait_recv()
    small = (iota((FIELDS, FIELDS), 0) == iota((FIELDS, FIELDS), 1)).astype(F32).astype(BF16)
    for start in range(0, asked, step):
        wanted = arrived[start // cap : (start + step) // cap].reshape(step, FIELDS)
        fields = lax.dot_general(small, wanted, NT, preferred_element_type=F32).astype(I32)
        valid = fields[subspaces + 2 : subspaces + 3, :] > 0
        slot = fields[subspaces : subspaces + 1, :] * 16 + fields[subspaces + 1 : subspaces + 2, :]
        asked_codes = fields[:subspaces, :]
        here = slice(rows + start, rows + start + step)
        high[:, here] = jnp.where(valid, asked_codes >> 5, top + 1).astype(F32)
        low[:, here] = (asked_codes & (LOW - 1)).astype(F32)
        pick = (iota((lists, step), 0) == slot).astype(F32).astype(BF16)
        parts[:, here] = (-jnp.dot(turned[...], pick, preferred_element_type=F32)).astype(BF16)

    def tab_peer(offset):
        return lax.rem(my_tab + offset, n_tab)

    def row_peer(offset):
        return lax.rem(my_row + offset, n_rows)

    def asked_group(index, carry):
        wide = pl.multiple_of(index * lines, lines)
        folded = sums[pl.ds(wide, lines), :] + fold(fill(index, rows, rows + asked), lines, sub_width)
        for m in range(group):
            subspace = index * group + m
            r, q = subspace // own, lax.rem(subspace, own)
            for half in range(codewords // 128):
                pieces[2 * q + half, r] = folded[
                    m * sub_width : (m + 1) * sub_width, half * 128 : (half + 1) * 128
                ].astype(BF16)
        return carry

    lax.fori_loop(0, subspaces // group, asked_group, 0)

    def copy1(source, slot, peer):
        return pltpu.make_async_remote_copy(
            src_ref=pieces.at[source], dst_ref=first.at[slot],
            send_sem=sent1.at[source], recv_sem=got1.at[slot],
            device_id=(my_row, peer), device_id_type=MESH,
        )

    def start1(offset, carry):
        copy1(tab_peer(offset), my_tab, tab_peer(offset)).start()
        return carry

    lax.fori_loop(1, n_tab, start1, 0)
    total[...] = pieces[my_tab].astype(F32)

    def add1(offset, carry):
        source = tab_peer(n_tab - offset)
        copy1(tab_peer(offset), source, tab_peer(offset)).wait_recv()
        total[...] += first[source].astype(F32)
        return carry

    lax.fori_loop(1, n_tab, add1, 0)
    middle[...] = total[...].astype(BF16)

    def copy2(source, slot, peer):
        return pltpu.make_async_remote_copy(
            src_ref=middle.at[source], dst_ref=second.at[slot],
            send_sem=sent2.at[source], recv_sem=got2.at[slot],
            device_id=(peer, my_tab), device_id_type=MESH,
        )

    def start2(offset, carry):
        copy2(row_peer(offset), my_row, row_peer(offset)).start()
        return carry

    lax.fori_loop(1, n_rows, start2, 0)

    def add2(offset, held):
        source = row_peer(n_rows - offset)
        copy2(row_peer(offset), source, row_peer(offset)).wait_recv()
        return held + second[source].astype(F32)

    mine[...] = lax.fori_loop(1, n_rows, add2, total[my_row])
    third[my_tab] = mine[...]

    def copy3(slot, peer):
        return pltpu.make_async_remote_copy(
            src_ref=mine, dst_ref=third.at[slot],
            send_sem=sent3.at[peer], recv_sem=got3.at[slot],
            device_id=(my_row, peer), device_id_type=MESH,
        )

    def start3(offset, carry):
        copy3(my_tab, tab_peer(offset)).start()
        return carry

    lax.fori_loop(1, n_tab, start3, 0)
    everything.wait_send()

    def drain_tab(offset, carry):
        copy1(tab_peer(offset), my_tab, tab_peer(offset)).wait_send()
        return carry

    def drain_row(offset, carry):
        copy2(row_peer(offset), my_row, row_peer(offset)).wait_send()
        return carry

    def wait3(offset, carry):
        copy3(tab_peer(n_tab - offset), tab_peer(offset)).wait_recv()
        copy3(my_tab, tab_peer(offset)).wait_send()
        return carry

    lax.fori_loop(1, n_tab, drain_tab, 0)
    lax.fori_loop(1, n_rows, drain_row, 0)
    lax.fori_loop(1, n_tab, wait3, 0)
    for q in range(own + 1):
        for half in range(codewords // 128):
            out_ref[q, :, half * 128 : (half + 1) * 128] = third[2 * q + half]


def totals(owner, slot, codes_t, vectors, centroids, rotation, codewords, n_rows, n_tab):
    subspaces, rows = codes_t.shape
    lists, width = centroids.shape
    own = subspaces // n_rows
    devices = n_rows * n_tab
    asked = 2 * rows
    every = rows + asked
    top = codewords // LOW
    lines = top * (width // subspaces)
    vmem, anywhere = pl.BlockSpec(memory_space=pltpu.VMEM), pl.BlockSpec(memory_space=pl.ANY)
    dma = pltpu.SemaphoreType.DMA
    return pl.pallas_call(
        functools.partial(fused_kernel, n_rows, n_tab),
        out_shape=jax.ShapeDtypeStruct((own + 1, 8, codewords), F32),
        in_specs=[vmem] * 3 + [anywhere] * 3,
        out_specs=vmem,
        scratch_shapes=[
            pltpu.VMEM((rows, width), BF16),
            pltpu.VMEM((lists, width), BF16),
            pltpu.VMEM((width, width), BF16),
            dma((3,)),
            pltpu.VMEM((devices, asked // devices, FIELDS), BF16),
            pltpu.VMEM((devices, asked // devices, FIELDS), BF16),
            dma,
            dma,
            pltpu.VMEM((width, codewords), F32),
            pltpu.VMEM((subspaces, codewords), F32),
            pltpu.VMEM((width, every), BF16),
            pltpu.VMEM((subspaces, every), F32),
            pltpu.VMEM((subspaces, every), F32),
            pltpu.VMEM((top * lines, every), BF16),
            pltpu.VMEM((codewords, every), BF16),
            pltpu.VMEM((width, lists), BF16),
            pltpu.VMEM((width, width), BF16),
            pltpu.VMEM((n_tab, n_rows, 8, 128), BF16),
            pltpu.VMEM((n_tab, n_rows, 8, 128), BF16),
            pltpu.VMEM((n_rows, 8, 128), F32),
            pltpu.VMEM((n_rows, 8, 128), BF16),
            pltpu.VMEM((n_rows, 8, 128), BF16),
            pltpu.VMEM((8, 128), F32),
            pltpu.VMEM((n_tab, 8, 128), F32),
            dma((n_tab,)),
            dma((n_tab,)),
            dma((n_rows,)),
            dma((n_rows,)),
            dma((n_tab,)),
            dma((n_tab,)),
        ],
        compiler_params=pltpu.CompilerParams(collective_id=0, has_side_effects=True),
    )(owner, slot, codes_t, vectors, centroids, rotation)


def body(vectors, list_owner, list_slot, codes, centroids, rotation, old_codebooks):
    n_rows = lax.axis_size("rows")
    n_tab = lax.axis_size("tab")
    row_dev = vectors.shape[0]
    own, _, codewords = old_codebooks.shape
    summed = totals(
        list_owner.reshape(1, row_dev),
        list_slot.reshape(1, row_dev),
        codes.T,
        vectors,
        centroids,
        rotation,
        codewords,
        n_rows,
        n_tab,
    )
    prior = float(row_dev * n_rows * n_tab // codewords)
    counts = summed[own, :own] + summed[own, own : 2 * own]
    return (summed[:own] + prior * old_codebooks) / (counts[:, None, :] + prior)


def solution(mesh):
    return jax.shard_map(
        body,
        mesh=mesh,
        in_specs=(
            P(("rows", "tab"), None),
            P(("rows", "tab"), None),
            P(("rows", "tab")),
            P(("rows", "tab"), None),
            P(("rows", "tab"), None),
            P(),
            P("rows", None, None),
        ),
        out_specs=P("rows", None, None),
        check_vma=False,
    )
```

```python
import functools

import jax
import jax.numpy as jnp
from jax import lax
from jax.experimental import pallas as pl
from jax.experimental.pallas import tpu as pltpu
from jax.sharding import PartitionSpec as P

FIELDS = 128
LOW = 32
UNITS = 3
PLANES = 8
BF16 = jnp.bfloat16
F32 = jnp.float32
I32 = jnp.int32
NT = (((1,), (1,)), ((), ()))
MESH = pl.DeviceIdType.MESH


def iota(shape, axis):
    return lax.broadcasted_iota(I32, shape, axis)


def fused_kernel(
    n_rows, n_tab, prior,
    owner_ref, slot_ref, codes_ref, old_ref, vectors_hbm, centroids_hbm, rotation_hbm,
    out_ref,
    vectors_ref, centroids_ref, rotation_ref, load_sem,
    message, arrived, sent_sem, got_sem,
    sums, tallies, parts, high, low, left, right, turned, flipped,
    pieces, first, total, middle, second, mine, third,
    sent1, got1, sent2, got2, sent3, got3,
):
    devices = n_rows * n_tab
    my_row, my_tab = lax.axis_index("rows"), lax.axis_index("tab")
    me = my_row * n_tab + my_tab
    barrier = pltpu.get_barrier_semaphore()

    loads = [
        pltpu.make_async_copy(source, target, load_sem.at[number])
        for number, (source, target) in enumerate(
            [(rotation_hbm, rotation_ref), (vectors_hbm, vectors_ref), (centroids_hbm, centroids_ref)]
        )
    ]
    for load in loads:
        load.start()

    def device(peer):
        return (peer // n_tab, lax.rem(peer, n_tab))

    def greet(offset, carry):
        pl.semaphore_signal(
            barrier, inc=1, device_id=device(lax.rem(me + offset, devices)), device_id_type=MESH
        )
        return carry

    lax.fori_loop(1, devices, greet, 0)

    subspaces, rows = codes_ref.shape
    cap = message.shape[1]
    owner = owner_ref[...]
    same = iota((devices, rows), 0) == owner
    before = (iota((rows, rows), 0) < iota((rows, rows), 1)).astype(F32).astype(BF16)
    rank = jnp.dot(same.astype(F32).astype(BF16), before, preferred_element_type=F32)
    rank = jnp.sum(jnp.where(same, rank, 0.0), axis=0, keepdims=True)
    place = owner * cap + rank.astype(I32)
    slot = slot_ref[...]
    line = iota((FIELDS - subspaces, rows), 0)
    extra = jnp.where(line == 0, slot >> 4, jnp.where(line == 1, slot & 15, (line == 2).astype(I32)))
    info = jnp.concatenate([codes_ref[...], extra], axis=0).astype(F32).astype(BF16)
    step = 256
    for start in range(0, devices * cap, step):
        hit = ((iota((step, rows), 0) + start) == place).astype(F32).astype(BF16)
        piece = lax.dot_general(hit, info, NT, preferred_element_type=F32).astype(BF16)
        message[start // cap : (start + step) // cap] = piece.reshape(step // cap, cap, FIELDS)

    plane = devices // PLANES
    block = 2 * plane
    my_plane, my_place = me // plane, lax.rem(me, plane)
    arrived[block - 1] = message[me]
    loads[0].wait()
    width = rotation_ref.shape[0]
    for start in range(0, width, 256):
        picker = ((iota((256, width), 0) + start) == iota((256, width), 1)).astype(F32).astype(BF16)
        flipped[start : start + 256, :] = lax.dot_general(
            picker, rotation_ref[...], NT, preferred_element_type=F32
        ).astype(BF16)
    pl.semaphore_wait(barrier, devices - 1)

    def ask(number, away, turn, at):
        peer = lax.rem(my_plane + away, PLANES) * plane + lax.rem(my_place + turn, plane)
        pltpu.make_async_remote_copy(
            src_ref=message.at[peer],
            dst_ref=arrived.at[number * block + at],
            send_sem=sent_sem,
            recv_sem=got_sem.at[number],
            device_id=device(peer),
            device_id_type=MESH,
        ).start()

    for number in range(PLANES // 2):

        def send(turn, carry, number=number):
            ask(number, PLANES // 2 - number, turn, turn)
            if number == 0:

                @pl.when(turn < plane - 1)
                def _():
                    ask(0, 0, turn + 1, plane + turn)
            else:
                ask(number, PLANES // 2 + number, turn, plane + turn)
            return carry

        lax.fori_loop(0, plane, send, 0)

    lists = centroids_ref.shape[0]
    asked = devices * cap
    sub_width = width // subspaces
    codewords = sums.shape[1]
    top = codewords // LOW
    group = codewords // LOW
    lines = group * sub_width
    own = subspaces // n_rows

    codes = codes_ref[...]
    high[:, :rows] = (codes >> 5).astype(F32)
    low[:, :rows] = (codes & (LOW - 1)).astype(F32)
    loads[1].wait()
    for start in range(0, rows, 256):
        parts[:, start : start + 256] = lax.dot_general(
            flipped[...], vectors_ref[start : start + 256, :], NT, preferred_element_type=F32
        ).astype(BF16)

    def fill(index, unit, begin, end, counted):
        line = pl.multiple_of(index * group, group)
        wide = pl.multiple_of(index * lines, lines)
        chunk = 512
        for start in range(begin, end, chunk):
            here = slice(start, start + chunk)
            there = slice(start - begin, start - begin + chunk)
            high8 = high[pl.ds(line, group), here]
            low8 = low[pl.ds(line, group), here]
            piece = parts[pl.ds(wide, lines), here]
            spread = jnp.concatenate(
                [jnp.broadcast_to(high8[m : m + 1], (sub_width, chunk)) for m in range(group)], axis=0
            ).astype(BF16)
            for value in range(top):
                left[unit, value * lines : (value + 1) * lines, there] = jnp.where(
                    spread == jnp.array(value, BF16), piece, jnp.zeros_like(piece)
                )
            if counted:
                left[unit, top * lines : top * (lines + group), there] = jnp.concatenate(
                    [jnp.where(high8 == float(value), 1.0, 0.0) for value in range(top)], axis=0
                ).astype(BF16)
            row_id = iota((LOW, chunk), 0).astype(F32).astype(BF16)
            for m in range(group):
                row = jnp.broadcast_to(low8[m : m + 1], (LOW, chunk)).astype(BF16)
                right[unit, m * LOW : (m + 1) * LOW, there] = jnp.where(
                    row == row_id, jnp.array(1, BF16), jnp.array(0, BF16)
                )

    def product(unit, depth, count):
        return lax.dot_general(
            left[unit, :count, :depth], right[unit, :, :depth], NT, preferred_element_type=F32
        )

    def fold(crossing, count, per):
        subspace = iota((count, 128), 0) // per
        quarter, lane = subspace & 3, iota((count, 128), 1) // LOW
        halves = []
        for half in range(codewords // 128):
            picked = [
                jnp.where(
                    subspace < 4,
                    crossing[value * count : (value + 1) * count, :128],
                    crossing[value * count : (value + 1) * count, 128:],
                )
                for value in range(4 * half, 4 * half + 4)
            ]
            moved = jnp.zeros((count, 128), F32)
            for turn in range(4):
                mixed = picked[0]
                for value in range(4):
                    mixed = jnp.where(lane == ((value - turn) & 3), picked[value], mixed)
                if turn:
                    mixed = pltpu.roll(mixed, LOW * turn, 1)
                moved = jnp.where(((lane - quarter) & 3) == turn, mixed, moved)
            halves.append(moved)
        return jnp.concatenate(halves, axis=1)

    def own_groups(index, carry):
        for unit in range(UNITS):
            fill(index * UNITS + unit, unit, 0, rows, True)
        for unit in range(UNITS):
            line = pl.multiple_of((index * UNITS + unit) * group, group)
            wide = pl.multiple_of((index * UNITS + unit) * lines, lines)
            crossed = product(unit, rows, top * (lines + group))
            sums[pl.ds(wide, lines), :] = fold(crossed[: top * lines], lines, sub_width)
            tallies[pl.ds(line, group), :] = fold(crossed[top * lines :], group, 1)
        return carry

    steps = subspaces // (group * UNITS)
    lax.fori_loop(0, steps, own_groups, 0)
    loads[2].wait()
    for start in range(0, lists, 256):
        turned[:, start : start + 256] = lax.dot_general(
            flipped[...], centroids_ref[start : start + 256, :], NT, preferred_element_type=F32
        ).astype(BF16)
    counts = tallies[...]
    coarse = jnp.floor(counts * (1 / 256)) * 256
    fine = counts - coarse
    gap = jnp.zeros((8 - 2 * own, 128), F32)
    for r in range(n_rows):
        these = slice(r * own, (r + 1) * own)
        for half in range(codewords // 128):
            lanes = slice(half * 128, (half + 1) * 128)
            pieces[2 * own + half, r] = jnp.concatenate(
                [coarse[these, lanes], fine[these, lanes], gap], axis=0
            ).astype(BF16)

    small = (iota((FIELDS, FIELDS), 0) == iota((FIELDS, FIELDS), 1)).astype(F32).astype(BF16)
    next_door = (my_row, lax.rem(my_tab + 1, n_tab))
    for number in range(PLANES // 2):
        count = block - 1 if number == 0 else block
        pltpu.make_async_remote_copy(
            src_ref=message.at[pl.ds(0, count)],
            dst_ref=arrived.at[pl.ds(number * block, count)],
            send_sem=sent_sem,
            recv_sem=got_sem.at[number],
            device_id=next_door,
            device_id_type=MESH,
        ).wait_recv()
        for start in range(number * block * cap, (number + 1) * block * cap, step):
            wanted = arrived[start // cap : (start + step) // cap].reshape(step, FIELDS)
            fields = lax.dot_general(small, wanted, NT, preferred_element_type=F32).astype(I32)
            valid = fields[subspaces + 2 : subspaces + 3, :] > 0
            slot = fields[subspaces : subspaces + 1, :] * 16 + fields[subspaces + 1 : subspaces + 2, :]
            asked_codes = fields[:subspaces, :]
            here = slice(rows + start, rows + start + step)
            high[:, here] = jnp.where(valid, asked_codes >> 5, top + 1).astype(F32)
            low[:, here] = (asked_codes & (LOW - 1)).astype(F32)
            pick = (iota((lists, step), 0) == slot).astype(F32).astype(BF16)
            parts[:, here] = (-jnp.dot(turned[...], pick, preferred_element_type=F32)).astype(BF16)

    def tab_peer(offset):
        return lax.rem(my_tab + offset, n_tab)

    def row_peer(offset):
        return lax.rem(my_row + offset, n_rows)

    share = n_rows // steps

    def copy1(index, source, slot, peer):
        rows_here = pl.ds(index * share, share)
        return pltpu.make_async_remote_copy(
            src_ref=pieces.at[source, rows_here], dst_ref=first.at[slot, rows_here],
            send_sem=sent1.at[index, source], recv_sem=got1.at[index, slot],
            device_id=(my_row, peer), device_id_type=MESH,
        )

    def asked_groups(index, carry):
        for unit in range(UNITS):
            fill(index * UNITS + unit, unit, rows, rows + asked, False)
        for unit in range(UNITS):
            wide = pl.multiple_of((index * UNITS + unit) * lines, lines)
            crossed = product(unit, asked, top * lines)
            folded = sums[pl.ds(wide, lines), :] + fold(crossed, lines, sub_width)
            for m in range(group):
                subspace = unit * group + m
                for half in range(codewords // 128):
                    pieces[2 * (subspace % own) + half, index * share + subspace // own] = folded[
                        m * sub_width : (m + 1) * sub_width, half * 128 : (half + 1) * 128
                    ].astype(BF16)
        for offset in range(1, n_tab):
            copy1(index, tab_peer(offset), my_tab, tab_peer(offset)).start()
        return carry

    lax.fori_loop(0, steps, asked_groups, 0)

    def copy2(source, slot, peer):
        return pltpu.make_async_remote_copy(
            src_ref=middle.at[source], dst_ref=second.at[slot],
            send_sem=sent2.at[source], recv_sem=got2.at[slot],
            device_id=(peer, my_tab), device_id_type=MESH,
        )

    def add1(index, carry):
        rows_here = pl.ds(index * share, share)
        added = pieces[my_tab, rows_here].astype(F32)
        for offset in range(1, n_tab):
            source = tab_peer(n_tab - offset)
            copy1(index, tab_peer(offset), source, tab_peer(offset)).wait_recv()
            added += first[source, rows_here].astype(F32)
        total[rows_here] = added
        middle[rows_here] = added.astype(BF16)
        for number in range(share):
            peer = index * share + number

            @pl.when(peer != my_row)
            def _():
                copy2(peer, my_row, peer).start()

        return carry

    lax.fori_loop(0, steps, add1, 0)

    def add2(offset, held):
        source = row_peer(n_rows - offset)
        copy2(row_peer(offset), source, row_peer(offset)).wait_recv()
        return held + second[source].astype(F32)

    mine[...] = lax.fori_loop(1, n_rows, add2, total[my_row])
    third[my_tab] = mine[...]

    def copy3(slot, peer):
        return pltpu.make_async_remote_copy(
            src_ref=mine, dst_ref=third.at[slot],
            send_sem=sent3.at[peer], recv_sem=got3.at[slot],
            device_id=(my_row, peer), device_id_type=MESH,
        )

    for offset in range(1, n_tab):
        copy3(my_tab, tab_peer(offset)).start()
    pltpu.make_async_remote_copy(
        src_ref=message.at[pl.ds(0, devices - 1)],
        dst_ref=arrived.at[pl.ds(0, devices - 1)],
        send_sem=sent_sem,
        recv_sem=got_sem.at[0],
        device_id=next_door,
        device_id_type=MESH,
    ).wait_send()

    def drain_tab(index, carry):
        for offset in range(1, n_tab):
            copy1(index, tab_peer(offset), my_tab, tab_peer(offset)).wait_send()
        return carry

    def drain_row(offset, carry):
        copy2(row_peer(offset), my_row, row_peer(offset)).wait_send()
        return carry

    lax.fori_loop(0, steps, drain_tab, 0)
    lax.fori_loop(1, n_rows, drain_row, 0)
    for offset in range(1, n_tab):
        copy3(tab_peer(n_tab - offset), tab_peer(offset)).wait_recv()
        copy3(my_tab, tab_peer(offset)).wait_send()
    for half in range(codewords // 128):
        lanes = slice(half * 128, (half + 1) * 128)
        counted = third[2 * own + half]
        for q in range(own):
            weight = counted[q : q + 1] + counted[own + q : own + q + 1] + prior
            out_ref[q, :, lanes] = (third[2 * q + half] + prior * old_ref[q, :, lanes]) / weight


def update(owner, slot, codes_t, old_codebooks, vectors, centroids, rotation, n_rows, n_tab):
    subspaces, rows = codes_t.shape
    lists, width = centroids.shape
    codewords = old_codebooks.shape[2]
    devices = n_rows * n_tab
    asked = 2 * rows
    every = rows + asked
    top = codewords // LOW
    lines = top * (width // subspaces)
    steps = subspaces // (top * UNITS)
    prior = float(rows * devices // codewords)
    vmem, anywhere = pl.BlockSpec(memory_space=pltpu.VMEM), pl.BlockSpec(memory_space=pl.ANY)
    dma = pltpu.SemaphoreType.DMA
    return pl.pallas_call(
        functools.partial(fused_kernel, n_rows, n_tab, prior),
        out_shape=jax.ShapeDtypeStruct(old_codebooks.shape, F32),
        in_specs=[vmem] * 4 + [anywhere] * 3,
        out_specs=vmem,
        scratch_shapes=[
            pltpu.VMEM((rows, width), BF16),
            pltpu.VMEM((lists, width), BF16),
            pltpu.VMEM((width, width), BF16),
            dma((3,)),
            pltpu.VMEM((devices, asked // devices, FIELDS), BF16),
            pltpu.VMEM((devices, asked // devices, FIELDS), BF16),
            dma,
            dma((PLANES // 2,)),
            pltpu.VMEM((width, codewords), F32),
            pltpu.VMEM((subspaces, codewords), F32),
            pltpu.VMEM((width, every), BF16),
            pltpu.VMEM((subspaces, every), F32),
            pltpu.VMEM((subspaces, every), F32),
            pltpu.VMEM((UNITS, top * (lines + top), asked), BF16),
            pltpu.VMEM((UNITS, codewords, asked), BF16),
            pltpu.VMEM((width, lists), BF16),
            pltpu.VMEM((width, width), BF16),
            pltpu.VMEM((n_tab, n_rows, 8, 128), BF16),
            pltpu.VMEM((n_tab, n_rows, 8, 128), BF16),
            pltpu.VMEM((n_rows, 8, 128), F32),
            pltpu.VMEM((n_rows, 8, 128), BF16),
            pltpu.VMEM((n_rows, 8, 128), BF16),
            pltpu.VMEM((8, 128), F32),
            pltpu.VMEM((n_tab, 8, 128), F32),
            dma((steps, n_tab)),
            dma((steps, n_tab)),
            dma((n_rows,)),
            dma((n_rows,)),
            dma((n_tab,)),
            dma((n_tab,)),
        ],
        compiler_params=pltpu.CompilerParams(collective_id=0, has_side_effects=True),
    )(owner, slot, codes_t, old_codebooks, vectors, centroids, rotation)


def body(vectors, list_owner, list_slot, codes, centroids, rotation, old_codebooks):
    row_dev = vectors.shape[0]
    return update(
        list_owner.reshape(1, row_dev),
        list_slot.reshape(1, row_dev),
        codes.T,
        old_codebooks,
        vectors,
        centroids,
        rotation,
        lax.axis_size("rows"),
        lax.axis_size("tab"),
    )


def solution(mesh):
    return jax.shard_map(
        body,
        mesh=mesh,
        in_specs=(
            P(("rows", "tab"), None),
            P(("rows", "tab"), None),
            P(("rows", "tab")),
            P(("rows", "tab"), None),
            P(("rows", "tab"), None),
            P(),
            P("rows", None, None),
        ),
        out_specs=P("rows", None, None),
        check_vma=False,
    )
```
